32 devices in a mesh: gx: 8 (over z, x), gy: 4 (over y, core).
Axes of the slice: x: 2, y: 2, z: 4, core: 2. Of those that a mesh axis runs over, the one named last changes fastest.
Arguments:
- velocity: float32 [3, 1, 1024, 2560], P(None, None, 'gy', 'gx'), may hold values from -12 to 12
- grid_x: float32 [33], replicated, may hold values from 0.05 to 1
- grid_y: float32 [1024, 33], P('gy'), may hold values from 0.05 to 1
- test_x: float32 [33], replicated, may hold values from 0.05 to 1
- test_y: float32 [1024, 33], P('gy'), may hold values from 0.05 to 1
Outputs:
- subgrid: float32 [6, 1, 1024, 2560], P(None, None, 'gy', 'gx')
- germano: float32 [6, 1, 1024, 2560], P(None, None, 'gy', 'gx')
The draws below stay inside these ranges and needn't reach their ends.
All inputs are finite; a program needn't handle non-finite values.
Results may differ from the reference program's by a relative error of at most 0.0001.
Values sent between devices are 32-bit elements; how exact they have to be, the bound alone decides.
A program may use at most 64 MiB of HBM per device.

```python
import math
import jax
import jax.numpy as jnp
from jax import lax

NZ = 1
TAPS = 33
NX = 2560
NY = 1024


def block_scale(key, dims, cuts, low, top_value):
    gain, own = 1.0, jax.random.fold_in(key, 6)
    for position, shards_of in cuts:
        draws = jnp.exp(jax.random.uniform(jax.random.fold_in(own, position), (shards_of,), jnp.float32, low / len(cuts), top_value / len(cuts)))
        gain = gain * jnp.repeat(draws, dims[position] // shards_of).reshape([-1 if axis == position else 1 for axis in range(len(dims))])
    return gain


def scatter_about(rng, extent, deviation, most, pieces=(), kind=jnp.bfloat16):
    level = block_scale(rng, extent, pieces, -0.22, 0.18) if pieces else 1.0
    values = jax.random.normal(rng, extent, jnp.float32) * deviation * level
    return jnp.minimum(jnp.maximum(values, -most), most).astype(kind)


def setup_inputs(seed: int = 0) -> dict:
    keys = jax.random.split(jax.random.key(seed), 6)
    return {
        "velocity": scatter_about(keys[0], (3, NZ, NY, NX), 2.0, 12.0, ((2, 4), (3, 8)), jnp.float32),
        "grid_x": jnp.clip(jnp.exp(jax.random.uniform(keys[1], (TAPS,), jnp.float32, math.log(0.05), math.log(1.0))), 0.05, 1.0),
        "grid_y": jnp.clip(jnp.exp(math.log(1.0) - 2.9957323 * jax.random.uniform(keys[2], (NY, TAPS), jnp.float32) ** block_scale(keys[2], (NY, TAPS), ((0, 4),), -0.2, 0.2)), 0.05, 1.0),
        "test_x": jnp.clip(jnp.exp(jax.random.uniform(keys[3], (TAPS,), jnp.float32, math.log(0.05), math.log(1.0))), 0.05, 1.0),
        "test_y": jnp.clip(jnp.exp(math.log(1.0) - 2.9957323 * jax.random.uniform(keys[4], (NY, TAPS), jnp.float32) ** block_scale(keys[4], (NY, TAPS), ((0, 4),), -0.2, 0.2)), 0.05, 1.0),
    }


COMPONENT_PAIRS = [(0, 0), (0, 1), (0, 2), (1, 1), (1, 2), (2, 2)]


def x_smooth(field, weights):
    taps_count = weights.shape[0]
    margin = (taps_count - 1) // 2
    normed = weights / jnp.sum(weights)
    padded = jnp.concatenate([field[..., -margin:], field, field[..., :margin]], axis=-1)
    lead_shape = field.shape[:-1]
    flat = padded.reshape((-1, 1, padded.shape[-1]))
    kernel = normed.reshape((1, 1, taps_count)).astype(field.dtype)
    result = lax.conv_general_dilated(flat, kernel, (1,), "VALID", precision=lax.Precision.HIGHEST)
    return result.reshape(lead_shape + (field.shape[-1],))


def y_smooth(field, table):
    rows_count = table.shape[0]
    taps_count = table.shape[1]
    margin = (taps_count - 1) // 2
    global_row = jnp.arange(rows_count, dtype=jnp.int32)
    source = global_row[:, None] + jnp.arange(taps_count, dtype=jnp.int32)[None, :] - margin
    inside = (source >= 0) & (source < rows_count)
    masked = jnp.where(inside, table, jnp.zeros_like(table))
    normed = masked / jnp.sum(masked, axis=1, keepdims=True)
    padded = jnp.pad(field, ((0, 0), (margin, margin), (0, 0)))
    result = jnp.zeros_like(field)
    for offset in range(taps_count):
        result = result + normed[:, offset][None, :, None] * padded[:, offset:offset + rows_count, :]
    return result


def smooth(field, weights, table):
    return y_smooth(x_smooth(field, weights), table)


def reference(velocity, grid_x, grid_y, test_x, test_y):
    coarse = [smooth(velocity[comp], grid_x, grid_y) for comp in range(3)]
    tested = [smooth(coarse[comp], test_x, test_y) for comp in range(3)]
    subgrid = []
    germano = []
    for first_comp, second_comp in COMPONENT_PAIRS:
        product = velocity[first_comp] * velocity[second_comp]
        subgrid.append(smooth(product, grid_x, grid_y) - coarse[first_comp] * coarse[second_comp])
        resolved = coarse[first_comp] * coarse[second_comp]
        germano.append(smooth(resolved, test_x, test_y) - tested[first_comp] * tested[second_comp])
    return jnp.stack(subgrid), jnp.stack(germano)
```

```python
import functools

import jax
import jax.numpy as jnp
from jax import lax
from jax.experimental import pallas as pl
from jax.experimental.pallas import tpu as pltpu
from jax.sharding import PartitionSpec as P

MESH = pl.DeviceIdType.MESH
LANES = 128
SUB = 8
DIRECTIONS = [(1, 0), (-1, 0), (0, 1), (0, -1), (1, 1), (-1, 1), (1, -1), (-1, -1)]
BF = jnp.bfloat16
F32 = jnp.float32


def round_up(value, unit):
    return (value + unit - 1) // unit * unit


def halo_kernel(nx, ny, width, v_ref, t_ref, ext_ref, text_ref,
                pack_l, pack_r, from_l, from_r, from_d, from_u, corners, t_low, t_high,
                send_sem, recv_sem):
    comps, rows, cols = v_ref.shape
    margin = t_low.shape[0]
    me_x, me_y = lax.axis_index("gx"), lax.axis_index("gy")

    def device(dx, dy):
        return {"gx": lax.rem(me_x + dx + nx, nx), "gy": lax.rem(me_y + dy + ny, ny)}

    barrier = pltpu.get_barrier_semaphore()
    for dx, dy in DIRECTIONS:
        pl.semaphore_signal(barrier, inc=1, device_id=device(dx, dy), device_id_type=MESH)

    per = LANES // width
    groups = rows // width
    for c in range(comps):
        for g in range(groups):
            for q in range(per):
                src = pl.ds(g * width + q * SUB, SUB)
                dst = pl.ds(g * SUB, SUB)
                pack_r[c, dst, q * width:(q + 1) * width] = v_ref[c, src, cols - width:cols]
                pack_l[c, dst, q * width:(q + 1) * width] = v_ref[c, src, 0:width]
    pl.semaphore_wait(barrier, len(DIRECTIONS))

    top = pl.ds((groups - 1) * SUB, SUB)
    low = pl.ds(0, SUB)
    sources = [
        pack_r, pack_l,
        v_ref.at[:, pl.ds(rows - width, width), :], v_ref.at[:, pl.ds(0, width), :],
        pack_r.at[:, top, :], pack_l.at[:, top, :], pack_r.at[:, low, :], pack_l.at[:, low, :],
    ]
    targets = [from_l, from_r, from_d, from_u] + [corners.at[i] for i in range(4)]
    copies = []
    for i, (dx, dy) in enumerate(DIRECTIONS):
        copies.append((dy, pltpu.make_async_remote_copy(
            src_ref=sources[i], dst_ref=targets[i], send_sem=send_sem.at[i],
            recv_sem=recv_sem.at[i], device_id=device(dx, dy), device_id_type=MESH)))
    for i, (dy, src, dst) in enumerate([
        (1, t_ref.at[pl.ds(rows - margin, margin), :], t_low),
        (-1, t_ref.at[pl.ds(0, margin), :], t_high),
    ]):
        n = len(DIRECTIONS) + i
        copies.append((dy, pltpu.make_async_remote_copy(
            src_ref=src, dst_ref=dst, send_sem=send_sem.at[n],
            recv_sem=recv_sem.at[n], device_id=device(0, dy), device_id_type=MESH)))

    has_up, has_down = me_y < ny - 1, me_y > 0
    for dy, copy in copies:
        if dy == 0:
            copy.start()
    for sign, present in ((1, has_up), (-1, has_down)):
        @pl.when(present)
        def _(sign=sign):
            for dy, copy in copies:
                if dy == sign:
                    copy.start()

    wide = ext_ref.shape[2]
    high = rows + width
    for c in range(comps):
        ext_ref[c, pl.ds(width, rows), width:width + cols] = v_ref[c]
    if wide > cols + 2 * width:
        ext_ref[:, :, cols + 2 * width:] = jnp.zeros(
            (comps, rows + 2 * width, wide - cols - 2 * width), F32)
    text_ref[...] = jnp.zeros_like(text_ref)
    text_ref[pl.ds(margin, rows), 0:t_ref.shape[1]] = t_ref[...]

    def unpack(buf, c, row, lane, count):
        for g in range(count):
            for q in range(per):
                ext_ref[c, pl.ds(row + g * width + q * SUB, SUB), lane:lane + width] = (
                    buf[c, pl.ds(g * SUB, SUB), q * width:(q + 1) * width])

    for sign, present, row, mid, pair, taps, trow in (
        (1, has_down, 0, from_d, (0, 1), t_low, 0),
        (-1, has_up, high, from_u, (2, 3), t_high, margin + rows),
    ):
        @pl.when(present)
        def _(sign=sign, row=row, mid=mid, pair=pair, taps=taps, trow=trow):
            for dy, copy in copies:
                if dy == sign:
                    copy.wait_recv()
            for c in range(comps):
                ext_ref[c, pl.ds(row, width), width:width + cols] = mid[c]
                unpack(corners.at[pair[0]], c, row, 0, 1)
                unpack(corners.at[pair[1]], c, row, width + cols, 1)
            text_ref[pl.ds(trow, margin), 0:t_ref.shape[1]] = taps[...]

        @pl.when(jnp.logical_not(present))
        def _(row=row):
            for c in range(comps):
                ext_ref[c, pl.ds(row, width), :] = jnp.zeros((width, wide), F32)

    copies[0][1].wait_recv()
    for c in range(comps):
        unpack(from_l, c, width, 0, groups)
    copies[1][1].wait_recv()
    for c in range(comps):
        unpack(from_r, c, width, width + cols, groups)

    for dy, copy in copies:
        if dy == 0:
            copy.wait_send()
    for sign, present in ((1, has_up), (-1, has_down)):
        @pl.when(present)
        def _(sign=sign):
            for dy, copy in copies:
                if dy == sign:
                    copy.wait_send()


def split(value):
    high = value.astype(BF)
    return high, (value - high.astype(F32)).astype(BF)


def pair_of(p):
    first = jnp.where(p < 3, 0, jnp.where(p < 5, 1, 2))
    second = jnp.where(p < 3, p, jnp.where(p < 5, p - 2, 2))
    return first, second


def stress_kernel(ny, taps, ext_ref, text_ref, gx_ref, tx_ref, ty_ref, sub_ref, ger_ref,
                  inner, coarse, coarse_in, tested, gxb, txb, gyb, gib, tyb, zh, zl):
    comps = ext_ref.shape[0]
    rows, cols = sub_ref.shape[1], sub_ref.shape[2]
    wide = ext_ref.shape[2]
    margin = (taps - 1) // 2
    rows_mid = rows + 2 * margin
    rows_ext = rows + 4 * margin
    first_row = lax.axis_index("gy") * rows
    total = rows * ny
    blk = LANES
    lane_tiles = wide // blk

    def skew(table):
        return pltpu.roll(table, 0, 1, stride=1, stride_axis=0)

    lane = lax.broadcasted_iota(jnp.int32, (blk, 2 * blk), 1)

    def x_band(w_ref, out):
        w = jnp.concatenate([w_ref[...], jnp.zeros((1, 2 * blk - w_ref.shape[1]), F32)], axis=1)
        w = w / jnp.sum(w)
        high, low = split(skew(jnp.broadcast_to(w, (blk, 2 * blk))))
        out[0], out[1] = high, low

    x_band(gx_ref, gxb)
    x_band(tx_ref, txb)

    def y_bands(load, row0, count, out):
        for n, start in enumerate(range(0, count, blk)):
            size = min(blk, count - start)
            raw = load(start, size)
            raw = jnp.concatenate([raw, jnp.zeros((size, 2 * blk - raw.shape[1]), F32)], axis=1)
            k = lax.broadcasted_iota(jnp.int32, (size, 2 * blk), 1)
            y = row0 + start + lax.broadcasted_iota(jnp.int32, (size, 2 * blk), 0)
            source = y + k - margin
            keep = (k < taps) & (source >= 0) & (source < total) & (y >= 0) & (y < total)
            w = jnp.where(keep, raw, 0.0)
            s = jnp.sum(w, axis=1, keepdims=True)
            w = w / jnp.where(s > 0.0, s, 1.0)
            high, low = split(skew(w))
            out[n, 0, 0:size], out[n, 1, 0:size] = high, low

    y_bands(lambda a, n: text_ref[pl.ds(a, n), :], first_row - margin, rows_mid, gyb)
    y_bands(lambda a, n: text_ref[pl.ds(a + margin, n), :], first_row, rows, gib)
    y_bands(lambda a, n: ty_ref[pl.ds(a, n), :], first_row, rows, tyb)

    def dot_t(a, b):
        return lax.dot_general(a, b, (((1,), (1,)), ((), ())), preferred_element_type=F32)

    def dot(a, b):
        return jnp.dot(a, b, preferred_element_type=F32)

    def filtered(load, rows_in, xb, yb, put):
        rows_out = rows_in - 2 * margin
        high, low = split(load())
        for t in range(lane_tiles):
            k0, k1 = t * blk, min((t + 2) * blk, wide)
            bh, bl = xb[0, :, 0:k1 - k0], xb[1, :, 0:k1 - k0]
            z = dot_t(high[:, k0:k1], bh) + dot_t(high[:, k0:k1], bl) + dot_t(low[:, k0:k1], bh)
            h, l = split(z)
            zh[0:rows_in, k0:k0 + blk] = h
            zl[0:rows_in, k0:k0 + blk] = l
        for n, start in enumerate(range(0, rows_out, blk)):
            size = min(blk, rows_out - start)
            k = size + 2 * margin
            bh, bl = yb[n, 0, 0:size, 0:k], yb[n, 1, 0:size, 0:k]
            dh, dl = zh[start:start + k, :], zl[start:start + k, :]
            put(start, size, dot(bh, dh) + dot(bl, dh) + dot(bh, dl))

    @pl.loop(0, comps)
    def _(c):
        inner[c] = pltpu.roll(ext_ref[c, pl.ds(margin, rows_mid), :], wide - margin, 1)

        def put(start, size, value):
            coarse[c, pl.ds(start, size), :] = value

        filtered(lambda: ext_ref[c], rows_ext, gxb, gyb, put)
        coarse_in[c] = pltpu.roll(coarse[c, pl.ds(margin, rows), :], wide - margin, 1)

        def put_tested(start, size, value):
            tested[c, pl.ds(start, size), :] = value

        filtered(lambda: coarse[c], rows_mid, txb, tyb, put_tested)

    @pl.loop(0, sub_ref.shape[0])
    def _(p):
        i, j = pair_of(p)

        def put_sub(start, size, value):
            at = pl.ds(start, size)
            sub_ref[p, at, :] = (value - coarse_in[i, at, :] * coarse_in[j, at, :])[:, 0:cols]

        filtered(lambda: inner[i] * inner[j], rows_mid, gxb, gib, put_sub)

        def put_ger(start, size, value):
            at = pl.ds(start, size)
            ger_ref[p, at, :] = (value - tested[i, at, :] * tested[j, at, :])[:, 0:cols]

        filtered(lambda: coarse[i] * coarse[j], rows_mid, txb, tyb, put_ger)


def local(nx, ny, velocity, grid_x, grid_y, test_x, test_y):
    comps, planes, rows, cols = velocity.shape
    taps = grid_x.shape[0]
    margin = (taps - 1) // 2
    width = 2 * margin
    wide = round_up(cols + 2 * width, LANES)
    pairs = comps * (comps + 1) // 2
    vmem = pl.BlockSpec(memory_space=pltpu.VMEM)
    packed = rows // width * SUB
    subs, gers = [], []
    rows_mid, rows_ext = rows + width, rows + 2 * width
    for plane in range(planes):
        v = velocity[:, plane]
        ext, text = pl.pallas_call(
            functools.partial(halo_kernel, nx, ny, width),
            out_shape=(
                jax.ShapeDtypeStruct((comps, rows_ext, wide), F32),
                jax.ShapeDtypeStruct((rows_mid, LANES), F32),
            ),
            in_specs=[vmem] * 2,
            out_specs=(vmem, vmem),
            scratch_shapes=[
                pltpu.VMEM((comps, packed, LANES), F32),
                pltpu.VMEM((comps, packed, LANES), F32),
                pltpu.VMEM((comps, packed, LANES), F32),
                pltpu.VMEM((comps, packed, LANES), F32),
                pltpu.VMEM((comps, width, cols), F32),
                pltpu.VMEM((comps, width, cols), F32),
                pltpu.VMEM((4, comps, SUB, LANES), F32),
                pltpu.VMEM((margin, taps), F32),
                pltpu.VMEM((margin, taps), F32),
                pltpu.SemaphoreType.DMA((len(DIRECTIONS) + 2,)),
                pltpu.SemaphoreType.DMA((len(DIRECTIONS) + 2,)),
            ],
            compiler_params=pltpu.CompilerParams(
                collective_id=plane, has_side_effects=True, vmem_limit_bytes=16 << 20),
            name="halo",
        )(v, grid_y)
        out = jax.ShapeDtypeStruct((pairs, rows, cols), F32)
        tiles_mid, tiles = pl.cdiv(rows_mid, LANES), pl.cdiv(rows, LANES)
        sub, ger = pl.pallas_call(
            functools.partial(stress_kernel, ny, taps),
            out_shape=(out, out),
            in_specs=[vmem] * 5,
            out_specs=(vmem, vmem),
            scratch_shapes=[
                pltpu.VMEM((comps, rows_mid, wide), F32),
                pltpu.VMEM((comps, rows_mid, wide), F32),
                pltpu.VMEM((comps, rows, wide), F32),
                pltpu.VMEM((comps, rows, wide), F32),
                pltpu.VMEM((2, LANES, 2 * LANES), BF),
                pltpu.VMEM((2, LANES, 2 * LANES), BF),
                pltpu.VMEM((tiles_mid, 2, LANES, 2 * LANES), BF),
                pltpu.VMEM((tiles, 2, LANES, 2 * LANES), BF),
                pltpu.VMEM((tiles, 2, LANES, 2 * LANES), BF),
                pltpu.VMEM((rows_ext, wide), BF),
                pltpu.VMEM((rows_ext, wide), BF),
            ],
            compiler_params=pltpu.CompilerParams(vmem_limit_bytes=40 << 20),
            name="stress",
        )(ext, text, grid_x.reshape(1, taps), test_x.reshape(1, taps), test_y)
        subs.append(sub)
        gers.append(ger)
    return jnp.stack(subs, axis=1), jnp.stack(gers, axis=1)


def solution(mesh):
    nx, ny = mesh.shape["gx"], mesh.shape["gy"]
    field = P(None, None, "gy", "gx")
    return jax.shard_map(
        functools.partial(local, nx, ny),
        mesh=mesh,
        in_specs=(field, P(), P("gy", None), P(), P("gy", None)),
        out_specs=(field, field),
        check_vma=False,
    )
```

```python
import functools

import jax
import jax.numpy as jnp
from jax import lax
from jax.experimental import pallas as pl
from jax.experimental.pallas import tpu as pltpu
from jax.sharding import PartitionSpec as P

MESH = pl.DeviceIdType.MESH
LANES = 128
SUB = 8
DIRECTIONS = [(1, 0), (-1, 0), (0, 1), (0, -1), (1, 1), (-1, 1), (1, -1), (-1, -1)]
BF = jnp.bfloat16
F32 = jnp.float32


def round_up(value, unit):
    return (value + unit - 1) // unit * unit


def halo_kernel(nx, ny, width, v_ref, t_ref, ext_ref, text_ref,
                pack_d, pack_u, from_d, from_u, from_l, from_r, corners, t_low, t_high,
                send_sem, recv_sem):
    comps, rows, cols = v_ref.shape
    taps = t_ref.shape[0]
    margin = width // 2
    me_x, me_y = lax.axis_index("gx"), lax.axis_index("gy")

    def device(dx, dy):
        return {"gx": lax.rem(me_x + dx + nx, nx), "gy": lax.rem(me_y + dy + ny, ny)}

    barrier = pltpu.get_barrier_semaphore()
    for dx, dy in DIRECTIONS:
        pl.semaphore_signal(barrier, inc=1, device_id=device(dx, dy), device_id_type=MESH)

    per = LANES // width
    groups = rows // width
    for c in range(comps):
        for g in range(groups):
            for q in range(per):
                src = pl.ds(g * width + q * SUB, SUB)
                dst = pl.ds(g * SUB, SUB)
                pack_u[c, dst, q * width:(q + 1) * width] = v_ref[c, src, cols - width:cols]
                pack_d[c, dst, q * width:(q + 1) * width] = v_ref[c, src, 0:width]
    pl.semaphore_wait(barrier, len(DIRECTIONS))

    first, last = pl.ds(0, SUB), pl.ds((groups - 1) * SUB, SUB)
    sources = [
        v_ref.at[:, pl.ds(rows - width, width), :], v_ref.at[:, pl.ds(0, width), :],
        pack_u, pack_d,
        pack_u.at[:, last, :], pack_u.at[:, first, :], pack_d.at[:, last, :], pack_d.at[:, first, :],
    ]
    targets = [from_l, from_r, from_d, from_u] + [corners.at[i] for i in range(4)]
    copies = []
    for i, (dx, dy) in enumerate(DIRECTIONS):
        copies.append((dy, pltpu.make_async_remote_copy(
            src_ref=sources[i], dst_ref=targets[i], send_sem=send_sem.at[i],
            recv_sem=recv_sem.at[i], device_id=device(dx, dy), device_id_type=MESH)))
    for i, (dy, src, dst) in enumerate([
        (1, t_ref.at[:, pl.ds(cols - LANES, LANES)], t_low),
        (-1, t_ref.at[:, pl.ds(0, LANES)], t_high),
    ]):
        n = len(DIRECTIONS) + i
        copies.append((dy, pltpu.make_async_remote_copy(
            src_ref=src, dst_ref=dst, send_sem=send_sem.at[n],
            recv_sem=recv_sem.at[n], device_id=device(0, dy), device_id_type=MESH)))

    has_up, has_down = me_y < ny - 1, me_y > 0
    for dy, copy in copies:
        if dy == 0:
            copy.start()
    for sign, present in ((1, has_up), (-1, has_down)):
        @pl.when(present)
        def _(sign=sign):
            for dy, copy in copies:
                if dy == sign:
                    copy.start()

    rows_ext = rows + 2 * width
    ext_ref[:, :, cols:] = jnp.zeros((comps, rows_ext, LANES), F32)
    text_ref[...] = jnp.zeros_like(text_ref)
    for c in range(comps):
        ext_ref[c, pl.ds(width, rows), 0:cols] = v_ref[c]
    text_ref[0:taps, 0:cols] = t_ref[...]

    def unpack(buf, c, row, lane, count):
        for g in range(count):
            for q in range(per):
                ext_ref[c, pl.ds(row + g * width + q * SUB, SUB), lane:lane + width] = (
                    buf[c, pl.ds(g * SUB, SUB), q * width:(q + 1) * width])

    for sign, present, lane, mid, pair, tile, at in (
        (1, has_down, cols + LANES - width, from_d, (0, 1), t_low, LANES - margin),
        (-1, has_up, cols, from_u, (2, 3), t_high, 0),
    ):
        @pl.when(present)
        def _(sign=sign, lane=lane, mid=mid, pair=pair, tile=tile, at=at):
            for dy, copy in copies:
                if dy == sign:
                    copy.wait_recv()
            for c in range(comps):
                unpack(mid, c, width, lane, groups)
                unpack(corners.at[pair[0]], c, 0, lane, 1)
                unpack(corners.at[pair[1]], c, width + rows, lane, 1)
            text_ref[0:taps, cols + at:cols + at + margin] = tile[:, at:at + margin]

    copies[0][1].wait_recv()
    for c in range(comps):
        ext_ref[c, pl.ds(0, width), 0:cols] = from_l[c]
    copies[1][1].wait_recv()
    for c in range(comps):
        ext_ref[c, pl.ds(width + rows, width), 0:cols] = from_r[c]

    for dy, copy in copies:
        if dy == 0:
            copy.wait_send()
    for sign, present in ((1, has_up), (-1, has_down)):
        @pl.when(present)
        def _(sign=sign):
            for dy, copy in copies:
                if dy == sign:
                    copy.wait_send()


def split(value):
    high = value.astype(BF)
    return high, (value - high.astype(F32)).astype(BF)


def pair_of(p):
    first = jnp.where(p < 3, 0, jnp.where(p < 5, 1, 2))
    second = jnp.where(p < 3, p, jnp.where(p < 5, p - 2, 2))
    return first, second


def dot(a, b):
    return jnp.dot(a, b, preferred_element_type=F32)


def x_weights(w_ref, step, out):
    taps = w_ref.shape[1]
    w = jnp.concatenate([w_ref[...], jnp.zeros((1, LANES - taps), F32)], axis=1)
    w = w / jnp.sum(w)
    band = pltpu.roll(jnp.broadcast_to(w, (LANES, LANES)), 0, 1, stride=1, stride_axis=0)
    high, low = split(band[0:step])
    out[0:step, 0:LANES] = high
    out[0:step, LANES:] = high
    out[step:, 0:LANES] = low
    out[step:, LANES:] = jnp.zeros((step, LANES), BF)


def y_weights(table, taps, first_row, total, cols, main, rest, edge=None):
    margin = (taps - 1) // 2
    lanes = table.shape[1]
    wide = cols + LANES
    k = lax.broadcasted_iota(jnp.int32, (LANES, lanes), 0)
    lane = lax.broadcasted_iota(jnp.int32, (LANES, lanes), 1)
    y = first_row + jnp.where(lane < cols + LANES // 2, lane, lane - wide)
    source = y + k - margin
    keep = (k < taps) & (source >= 0) & (source < total) & (y >= 0) & (y < total)
    w = jnp.where(keep, jnp.concatenate(
        [table, jnp.zeros((LANES - table.shape[0], lanes), F32)], axis=0), 0.0)
    s = jnp.sum(w, axis=0, keepdims=True)
    w = (w / jnp.where(s > 0.0, s, 1.0)).T
    zeros = jnp.zeros((LANES, cols), F32)
    for t in range(lanes // LANES):
        at = slice(t * LANES, (t + 1) * LANES)
        tile = jnp.concatenate([w[at], zeros], axis=1)
        band = pltpu.roll(tile, (t * LANES - margin) % wide, 1, stride=1, stride_axis=0)
        if t * LANES < cols:
            own, halo = band[:, 0:cols].T, band[:, cols:]
            main[0, :, at], main[1, :, at] = split(own)
            high = halo.astype(BF).astype(F32)
            packed = high + pltpu.roll(high, 2 * margin, 1) + pltpu.roll(halo - high, 4 * margin, 1)
            rest[:, at] = packed.T.astype(BF)
        elif edge is not None:
            edge[0], edge[1] = split(band.T)


def y_filter(load, margin, cols, main, rest, put, edge=None):
    value = load()
    high, low = split(value[:, 0:cols])
    halo = value[:, cols:]
    lane = lax.broadcasted_iota(jnp.int32, halo.shape, 1)
    near = jnp.where((lane < margin) | (lane >= LANES - margin), halo, 0.0)
    near_high = near.astype(BF).astype(F32)
    packed = near_high + pltpu.roll(near - near_high, 2 * margin, 1) + pltpu.roll(near_high, 4 * margin, 1)
    z = (dot(high, main[0]) + dot(high, main[1]) + dot(low, main[0])
         + dot(packed.astype(BF), rest[...]))
    put(z, slice(0, cols))
    if edge is not None:
        hh, hl = split(halo)
        z = (dot(high, edge[0, 0:cols]) + dot(high, edge[1, 0:cols]) + dot(low, edge[0, 0:cols])
             + dot(hh, edge[0, cols:]) + dot(hh, edge[1, cols:]) + dot(hl, edge[0, cols:]))
        put(z, slice(cols, cols + LANES))


def x_filter(zh, zl, start, count, lanes, weights, put):
    step = weights.shape[0] // 2
    for s in range(0, count, step):
        size = min(step, count - s)
        at = slice(start + s, start + s + LANES)
        data = jnp.concatenate([zh[at, lanes], zl[at, lanes]], axis=0)
        if size == step:
            r = dot(weights[...], data)
        else:
            r = dot(jnp.concatenate([weights[0:size], weights[step:step + size]], axis=0), data)
        put(s, size, r[0:size] + r[size:])


def stress_kernel(ny, taps, ext_ref, text_ref, gx_ref, tx_ref, ty_ref, sub_ref, ger_ref,
                  coarse, tested, sub, ger, gxw, txw, gym, gyr, gye, tym, tyr, zh, zl, sems):
    comps, rows_ext, wide = ext_ref.shape
    pairs, rows, cols = sub_ref.shape
    margin = (taps - 1) // 2
    rows_mid = rows + 2 * margin
    first_row = lax.axis_index("gy") * cols
    total = cols * ny

    x_weights(gx_ref, gxw.shape[0] // 2, gxw)
    x_weights(tx_ref, txw.shape[0] // 2, txw)
    y_weights(text_ref[...], taps, first_row, total, cols, gym, gyr, gye)
    y_weights(ty_ref[...], taps, first_row, total, cols, tym, tyr)
    zh[pl.ds(rows_ext, LANES), :] = jnp.zeros((LANES, wide), BF)
    zl[pl.ds(rows_ext, LANES), :] = jnp.zeros((LANES, wide), BF)
    own = slice(0, cols)
    everything = slice(0, wide)

    def store(count):
        def put(z, lanes):
            zh[0:count, lanes], zl[0:count, lanes] = split(z)
        return put

    @pl.loop(0, comps)
    def _(c):
        y_filter(lambda: ext_ref[c], margin, cols, gym, gyr, store(rows_ext), gye)

        def put(start, size, value):
            coarse[c, pl.ds(start, size), :] = value

        x_filter(zh, zl, 0, rows_mid, everything, gxw, put)
        y_filter(lambda: coarse[c], margin, cols, tym, tyr, store(rows_mid))

        def put_tested(start, size, value):
            tested[c, pl.ds(start, size), :] = value

        x_filter(zh, zl, 0, rows, own, txw, put_tested)

    def leave(which, source, target, p):
        return pltpu.make_async_copy(source.at[p], target.at[p], sems.at[which, p])

    @pl.loop(0, pairs)
    def _(p):
        i, j = pair_of(p)
        mid = pl.ds(margin, rows_mid)
        y_filter(lambda: ext_ref[i, mid, :] * ext_ref[j, mid, :], margin, cols, gym, gyr,
                 store(rows_mid))

        def put_sub(start, size, value):
            at = pl.ds(margin + start, size)
            sub[p, pl.ds(start, size), :] = value - coarse[i, at, own] * coarse[j, at, own]

        x_filter(zh, zl, 0, rows, own, gxw, put_sub)
        leave(0, sub, sub_ref, p).start()

        y_filter(lambda: coarse[i] * coarse[j], margin, cols, tym, tyr, store(rows_mid))

        def put_ger(start, size, value):
            at = pl.ds(start, size)
            ger[p, at, :] = value - tested[i, at, :] * tested[j, at, :]

        x_filter(zh, zl, 0, rows, own, txw, put_ger)
        leave(1, ger, ger_ref, p).start()

    @pl.loop(0, pairs)
    def _(p):
        leave(0, sub, sub_ref, p).wait()
        leave(1, ger, ger_ref, p).wait()


def local(nx, ny, velocity, grid_x, grid_y, test_x, test_y):
    comps, planes, cols, rows = velocity.shape
    taps = grid_x.shape[0]
    margin = (taps - 1) // 2
    width = 2 * margin
    wide = cols + LANES
    step = LANES - width
    pairs = comps * (comps + 1) // 2
    vmem = pl.BlockSpec(memory_space=pltpu.VMEM)
    anywhere = pl.BlockSpec(memory_space=pl.ANY)
    packed = rows // width * SUB
    subs, gers = [], []
    rows_mid, rows_ext = rows + width, rows + 2 * width
    for plane in range(planes):
        v = jnp.swapaxes(velocity[:, plane], 1, 2)
        ext, text = pl.pallas_call(
            functools.partial(halo_kernel, nx, ny, width),
            out_shape=(
                jax.ShapeDtypeStruct((comps, rows_ext, wide), F32),
                jax.ShapeDtypeStruct((round_up(taps, SUB), wide), F32),
            ),
            in_specs=[vmem] * 2,
            out_specs=(vmem, vmem),
            scratch_shapes=[
                pltpu.VMEM((comps, packed, LANES), F32),
                pltpu.VMEM((comps, packed, LANES), F32),
                pltpu.VMEM((comps, packed, LANES), F32),
                pltpu.VMEM((comps, packed, LANES), F32),
                pltpu.VMEM((comps, width, cols), F32),
                pltpu.VMEM((comps, width, cols), F32),
                pltpu.VMEM((4, comps, SUB, LANES), F32),
                pltpu.VMEM((taps, LANES), F32),
                pltpu.VMEM((taps, LANES), F32),
                pltpu.SemaphoreType.DMA((len(DIRECTIONS) + 2,)),
                pltpu.SemaphoreType.DMA((len(DIRECTIONS) + 2,)),
            ],
            compiler_params=pltpu.CompilerParams(
                collective_id=plane, has_side_effects=True, vmem_limit_bytes=16 << 20),
            name="halo",
        )(v, grid_y.T)
        out = jax.ShapeDtypeStruct((pairs, rows, cols), F32)
        sub, ger = pl.pallas_call(
            functools.partial(stress_kernel, ny, taps),
            out_shape=(out, out),
            in_specs=[vmem] * 5,
            out_specs=(anywhere, anywhere),
            scratch_shapes=[
                pltpu.VMEM((comps, rows_mid, wide), F32),
                pltpu.VMEM((comps, rows, cols), F32),
                pltpu.VMEM((pairs, rows, cols), F32),
                pltpu.VMEM((pairs, rows, cols), F32),
                pltpu.VMEM((2 * step, 2 * LANES), BF),
                pltpu.VMEM((2 * step, 2 * LANES), BF),
                pltpu.VMEM((2, cols, cols), BF),
                pltpu.VMEM((LANES, cols), BF),
                pltpu.VMEM((2, wide, LANES), BF),
                pltpu.VMEM((2, cols, cols), BF),
                pltpu.VMEM((LANES, cols), BF),
                pltpu.VMEM((rows_ext + LANES, wide), BF),
                pltpu.VMEM((rows_ext + LANES, wide), BF),
                pltpu.SemaphoreType.DMA((2, pairs)),
            ],
            compiler_params=pltpu.CompilerParams(vmem_limit_bytes=48 << 20),
            name="stress",
        )(ext, text, grid_x.reshape(1, taps), test_x.reshape(1, taps), test_y.T)
        subs.append(jnp.swapaxes(sub, 1, 2))
        gers.append(jnp.swapaxes(ger, 1, 2))
    return jnp.stack(subs, axis=1), jnp.stack(gers, axis=1)


def solution(mesh):
    nx, ny = mesh.shape["gx"], mesh.shape["gy"]
    field = P(None, None, "gy", "gx")
    return jax.shard_map(
        functools.partial(local, nx, ny),
        mesh=mesh,
        in_specs=(field, P(), P("gy", None), P(), P("gy", None)),
        out_specs=(field, field),
        check_vma=False,
    )
```

```python
import functools

import jax
import jax.numpy as jnp
from jax import lax
from jax.experimental import pallas as pl
from jax.experimental.pallas import tpu as pltpu
from jax.sharding import PartitionSpec as P

MESH = pl.DeviceIdType.MESH
LANES = 128
SUB = 8
DIRECTIONS = [(1, 0), (-1, 0), (0, 1), (0, -1), (1, 1), (-1, 1), (1, -1), (-1, -1)]
BF = jnp.bfloat16
F32 = jnp.float32


def round_up(value, unit):
    return (value + unit - 1) // unit * unit


def split(value):
    high = value.astype(BF)
    return high, (value - high.astype(F32)).astype(BF)


def pair_of(p):
    first = jnp.where(p < 3, 0, jnp.where(p < 5, 1, 2))
    second = jnp.where(p < 3, p, jnp.where(p < 5, p - 2, 2))
    return first, second


def dot(a, b):
    return jnp.dot(a, b, preferred_element_type=F32)


def x_weights(w_ref, step, out):
    taps = w_ref.shape[1]
    w = jnp.concatenate([w_ref[...], jnp.zeros((1, LANES - taps), F32)], axis=1)
    w = w / jnp.sum(w)
    band = pltpu.roll(jnp.broadcast_to(w, (LANES, LANES)), 0, 1, stride=1, stride_axis=0)
    high, low = split(band[0:step])
    out[0:step, 0:LANES] = high
    out[0:step, LANES:] = high
    out[step:, 0:LANES] = low
    out[step:, LANES:] = jnp.zeros((step, LANES), BF)


def y_weights(table, taps, first_row, total, cols, main, edge=None, tiles=None):
    margin = (taps - 1) // 2
    lanes = table.shape[1]
    wide = cols + LANES
    k = lax.broadcasted_iota(jnp.int32, (LANES, lanes), 0)
    lane = lax.broadcasted_iota(jnp.int32, (LANES, lanes), 1)
    y = first_row + jnp.where(lane < cols + LANES // 2, lane, lane - wide)
    source = y + k - margin
    keep = (k < taps) & (source >= 0) & (source < total) & (y >= 0) & (y < total)
    w = jnp.where(keep, jnp.concatenate(
        [table, jnp.zeros((LANES - table.shape[0], lanes), F32)], axis=0), 0.0)
    s = jnp.sum(w, axis=0, keepdims=True)
    w = (w / jnp.where(s > 0.0, s, 1.0)).T
    zeros = jnp.zeros((LANES, cols), F32)
    for t in (range(lanes // LANES) if tiles is None else tiles):
        at = slice(t * LANES, (t + 1) * LANES)
        tile = jnp.concatenate([w[at], zeros], axis=1)
        band = pltpu.roll(tile, (t * LANES - margin) % wide, 1, stride=1, stride_axis=0)
        if t * LANES < cols:
            own, halo = band[:, 0:cols].T, band[:, cols:]
            own_high, own_low = split(own)
            main[0:cols, at] = own_high
            main[cols:2 * cols, at] = own_low
            main[2 * cols:3 * cols, at] = own_high
            high = halo.astype(BF).astype(F32)
            packed = high + pltpu.roll(high, 2 * margin, 1) + pltpu.roll(halo - high, 4 * margin, 1)
            main[3 * cols:, at] = packed.T.astype(BF)
        else:
            edge_high, edge_low = split(band.T)
            at = 0
            for lo, hi in ((0, cols), (cols, wide)):
                for part in (edge_high, edge_low, edge_high):
                    edge[at:at + hi - lo] = part[lo:hi]
                    at += hi - lo


def halo_kernel(nx, ny, width, v_hbm, t_hbm, gx_hbm, tx_hbm, ty_hbm,
                ext_ref, gxw, txw, gym, gye, tym,
                v_ref, t_ref, gx_ref, tx_ref, ty_ref, text_ref, load_sem, pack_d, pack_u, from_d, from_u, from_l, from_r, corners, t_low, t_high,
                send_sem, recv_sem):
    comps, rows, cols = v_ref.shape
    taps = t_ref.shape[0]
    margin = width // 2
    me_x, me_y = lax.axis_index("gx"), lax.axis_index("gy")

    def device(dx, dy):
        return {"gx": lax.rem(me_x + dx + nx, nx), "gy": lax.rem(me_y + dy + ny, ny)}

    barrier = pltpu.get_barrier_semaphore()
    for dx, dy in DIRECTIONS:
        pl.semaphore_signal(barrier, inc=1, device_id=device(dx, dy), device_id_type=MESH)

    loads = [pltpu.make_async_copy(src, dst, load_sem.at[i]) for i, (src, dst) in enumerate((
        (v_hbm, v_ref), (t_hbm, t_ref), (gx_hbm, gx_ref), (tx_hbm, tx_ref), (ty_hbm, ty_ref)))]
    for load in loads:
        load.start()
    per = LANES // width
    groups = rows // width
    loads[0].wait()
    for c in range(comps):
        for g in range(groups):
            for q in range(per):
                src = pl.ds(g * width + q * SUB, SUB)
                dst = pl.ds(g * SUB, SUB)
                pack_u[c, dst, q * width:(q + 1) * width] = v_ref[c, src, cols - width:cols]
                pack_d[c, dst, q * width:(q + 1) * width] = v_ref[c, src, 0:width]
    pl.semaphore_wait(barrier, len(DIRECTIONS))

    loads[1].wait()
    first, last = pl.ds(0, SUB), pl.ds((groups - 1) * SUB, SUB)
    sources = [
        v_hbm.at[:, pl.ds(rows - width, width), :], v_hbm.at[:, pl.ds(0, width), :],
        pack_u, pack_d,
        pack_u.at[:, last, :], pack_u.at[:, first, :], pack_d.at[:, last, :], pack_d.at[:, first, :],
    ]
    targets = [from_l, from_r, from_d, from_u] + [corners.at[i] for i in range(4)]
    copies = []
    for i, (dx, dy) in enumerate(DIRECTIONS):
        copies.append((dy, pltpu.make_async_remote_copy(
            src_ref=sources[i], dst_ref=targets[i], send_sem=send_sem.at[i],
            recv_sem=recv_sem.at[i], device_id=device(dx, dy), device_id_type=MESH)))
    for i, (dy, src, dst) in enumerate([
        (1, t_ref.at[:, pl.ds(cols - LANES, LANES)], t_low),
        (-1, t_ref.at[:, pl.ds(0, LANES)], t_high),
    ]):
        n = len(DIRECTIONS) + i
        copies.append((dy, pltpu.make_async_remote_copy(
            src_ref=src, dst_ref=dst, send_sem=send_sem.at[n],
            recv_sem=recv_sem.at[n], device_id=device(0, dy), device_id_type=MESH)))

    has_up, has_down = me_y < ny - 1, me_y > 0
    for dy, copy in copies:
        if dy == 0:
            copy.start()
    for sign, present in ((1, has_up), (-1, has_down)):
        @pl.when(present)
        def _(sign=sign):
            for dy, copy in copies:
                if dy == sign:
                    copy.start()

    rows_ext = rows + 2 * width
    ext_ref[:, :, cols:] = jnp.zeros((comps, rows_ext, LANES), F32)
    text_ref[...] = jnp.zeros_like(text_ref)
    for c in range(comps):
        ext_ref[c, pl.ds(width, rows), 0:cols] = v_ref[c]
    text_ref[0:taps, 0:cols] = t_ref[...]
    for load in loads[2:]:
        load.wait()
    first_row, total = me_y * cols, cols * ny
    x_weights(gx_ref, gxw.shape[0] // 2, gxw)
    x_weights(tx_ref, txw.shape[0] // 2, txw)
    own_tiles = range(cols // LANES)
    y_weights(t_ref[...], taps, first_row, total, cols, gym, tiles=own_tiles)
    y_weights(ty_ref[...], taps, first_row, total, cols, tym, tiles=own_tiles)

    def unpack(buf, c, row, lane, count):
        for g in range(count):
            for q in range(per):
                ext_ref[c, pl.ds(row + g * width + q * SUB, SUB), lane:lane + width] = (
                    buf[c, pl.ds(g * SUB, SUB), q * width:(q + 1) * width])

    for sign, present, lane, mid, pair, tile, at in (
        (1, has_down, cols + LANES - width, from_d, (0, 1), t_low, LANES - margin),
        (-1, has_up, cols, from_u, (2, 3), t_high, 0),
    ):
        @pl.when(present)
        def _(sign=sign, lane=lane, mid=mid, pair=pair, tile=tile, at=at):
            for dy, copy in copies:
                if dy == sign:
                    copy.wait_recv()
            for c in range(comps):
                unpack(mid, c, width, lane, groups)
                unpack(corners.at[pair[0]], c, 0, lane, 1)
                unpack(corners.at[pair[1]], c, width + rows, lane, 1)
            text_ref[0:taps, cols + at:cols + at + margin] = tile[:, at:at + margin]

    y_weights(text_ref[...], taps, first_row, total, cols, gym, gye, tiles=(cols // LANES,))
    copies[0][1].wait_recv()
    for c in range(comps):
        ext_ref[c, pl.ds(0, width), 0:cols] = from_l[c]
    copies[1][1].wait_recv()
    for c in range(comps):
        ext_ref[c, pl.ds(width + rows, width), 0:cols] = from_r[c]

    for dy, copy in copies:
        if dy == 0:
            copy.wait_send()
    for sign, present in ((1, has_up), (-1, has_down)):
        @pl.when(present)
        def _(sign=sign):
            for dy, copy in copies:
                if dy == sign:
                    copy.wait_send()


def y_filter(value, margin, cols, main, put, edge=None):
    high, low = split(value[:, 0:cols])
    halo = value[:, cols:]
    lane = lax.broadcasted_iota(jnp.int32, halo.shape, 1)
    near = jnp.where((lane < margin) | (lane >= LANES - margin), halo, 0.0)
    near_high = near.astype(BF).astype(F32)
    packed = near_high + pltpu.roll(near - near_high, 2 * margin, 1) + pltpu.roll(near_high, 4 * margin, 1)
    put(dot(jnp.concatenate([high, high, low, packed.astype(BF)], axis=1), main[...]), slice(0, cols))
    if edge is not None:
        hh, hl = split(halo)
        put(dot(jnp.concatenate([high, high, low, hh, hh, hl], axis=1), edge[...]),
            slice(cols, cols + LANES))


def x_filter(zh, zl, start, count, lanes, weights, put):
    step = weights.shape[0] // 2
    for s in range(0, count, step):
        size = min(step, count - s)
        at = slice(start + s, start + s + LANES)
        data = jnp.concatenate([zh[at, lanes], zl[at, lanes]], axis=0)
        if size == step:
            r = dot(weights[...], data)
        else:
            r = dot(jnp.concatenate([weights[0:size], weights[step:step + size]], axis=0), data)
        put(s, size, r[0:size] + r[size:])


def stress_kernel(margin, batch, ext_ref, gxw, txw, gym, gye, tym, sub_ref, ger_ref,
                  coarse, tested, sub, ger, zh, zl, sems):
    comps, rows_ext, wide = ext_ref.shape
    pairs, rows, cols = sub_ref.shape
    rows_mid = rows + 2 * margin
    own = slice(0, cols)
    everything = slice(0, wide)
    for slot in range(zh.shape[0]):
        zh[slot, pl.ds(rows_ext, LANES), :] = jnp.zeros((LANES, wide), BF)
        zl[slot, pl.ds(rows_ext, LANES), :] = jnp.zeros((LANES, wide), BF)

    def store(slot, n, count):
        def put(z, lanes):
            high, low = split(z)
            for b in range(n):
                at = slice(b * count, (b + 1) * count)
                zh[slot + b, 0:count, lanes], zl[slot + b, 0:count, lanes] = high[at], low[at]
        return put

    def stacked(values):
        return jnp.concatenate(values, axis=0)

    y_filter(stacked([ext_ref[c] for c in range(comps)]), margin, cols, gym,
             store(0, comps, rows_ext), gye)
    for c in range(comps):
        def put(start, size, value, c=c):
            coarse[c, pl.ds(start, size), :] = value

        x_filter(zh.at[c], zl.at[c], 0, rows_mid, everything, gxw, put)
    y_filter(stacked([coarse[c] for c in range(comps)]), margin, cols, tym,
             store(0, comps, rows_mid))
    for c in range(comps):
        def put_tested(start, size, value, c=c):
            tested[c, pl.ds(start, size), :] = value

        x_filter(zh.at[c], zl.at[c], 0, rows, own, txw, put_tested)

    def leave(which, source, target, p):
        return pltpu.make_async_copy(source.at[p], target.at[p], sems.at[which, p])

    mid = pl.ds(margin, rows_mid)

    @pl.loop(0, pairs // batch)
    def _(step):
        indices = [(step * batch + b,) + pair_of(step * batch + b) for b in range(batch)]
        y_filter(stacked([ext_ref[i, mid, :] * ext_ref[j, mid, :] for _, i, j in indices]),
                 margin, cols, gym, store(0, batch, rows_mid))
        y_filter(stacked([coarse[i] * coarse[j] for _, i, j in indices]),
                 margin, cols, tym, store(batch, batch, rows_mid))
        for b, (p, i, j) in enumerate(indices):
            def put_sub(start, size, value, p=p, i=i, j=j):
                at = pl.ds(margin + start, size)
                sub[p, pl.ds(start, size), :] = value - coarse[i, at, own] * coarse[j, at, own]

            x_filter(zh.at[b], zl.at[b], 0, rows, own, gxw, put_sub)
        for b, (p, i, j) in enumerate(indices):
            def put_ger(start, size, value, p=p, i=i, j=j):
                at = pl.ds(start, size)
                ger[p, at, :] = value - tested[i, at, :] * tested[j, at, :]

            x_filter(zh.at[batch + b], zl.at[batch + b], 0, rows, own, txw, put_ger)
        for p, _, _ in indices:
            leave(0, sub, sub_ref, p).start()
            leave(1, ger, ger_ref, p).start()

    @pl.loop(0, pairs)
    def _(p):
        leave(0, sub, sub_ref, p).wait()
        leave(1, ger, ger_ref, p).wait()


def local(nx, ny, velocity, grid_x, grid_y, test_x, test_y):
    comps, planes, cols, rows = velocity.shape
    taps = grid_x.shape[0]
    margin = (taps - 1) // 2
    width = 2 * margin
    wide = cols + LANES
    step = LANES - width
    pairs = comps * (comps + 1) // 2
    batch = 2
    slots = max(comps, 2 * batch)
    vmem = pl.BlockSpec(memory_space=pltpu.VMEM)
    anywhere = pl.BlockSpec(memory_space=pl.ANY)
    packed = rows // width * SUB
    subs, gers = [], []
    rows_mid, rows_ext = rows + width, rows + 2 * width
    for plane in range(planes):
        v = jnp.swapaxes(velocity[:, plane], 1, 2)
        ext, *weights = pl.pallas_call(
            functools.partial(halo_kernel, nx, ny, width),
            out_shape=(
                jax.ShapeDtypeStruct((comps, rows_ext, wide), F32),
                jax.ShapeDtypeStruct((2 * step, 2 * LANES), BF),
                jax.ShapeDtypeStruct((2 * step, 2 * LANES), BF),
                jax.ShapeDtypeStruct((3 * cols + LANES, cols), BF),
                jax.ShapeDtypeStruct((3 * wide, LANES), BF),
                jax.ShapeDtypeStruct((3 * cols + LANES, cols), BF),
            ),
            in_specs=[pl.BlockSpec(memory_space=pltpu.HBM)] * 5,
            out_specs=(vmem,) * 6,
            scratch_shapes=[
                pltpu.VMEM((comps, rows, cols), F32),
                pltpu.VMEM((taps, cols), F32),
                pltpu.VMEM((1, taps), F32),
                pltpu.VMEM((1, taps), F32),
                pltpu.VMEM((taps, cols), F32),
                pltpu.VMEM((round_up(taps, SUB), wide), F32),
                pltpu.SemaphoreType.DMA((5,)),
                pltpu.VMEM((comps, packed, LANES), F32),
                pltpu.VMEM((comps, packed, LANES), F32),
                pltpu.VMEM((comps, packed, LANES), F32),
                pltpu.VMEM((comps, packed, LANES), F32),
                pltpu.VMEM((comps, width, cols), F32),
                pltpu.VMEM((comps, width, cols), F32),
                pltpu.VMEM((4, comps, SUB, LANES), F32),
                pltpu.VMEM((taps, LANES), F32),
                pltpu.VMEM((taps, LANES), F32),
                pltpu.SemaphoreType.DMA((len(DIRECTIONS) + 2,)),
                pltpu.SemaphoreType.DMA((len(DIRECTIONS) + 2,)),
            ],
            compiler_params=pltpu.CompilerParams(
                collective_id=plane, has_side_effects=True, vmem_limit_bytes=48 << 20),
            name="halo",
        )(*[pltpu.with_memory_space_constraint(x, pltpu.HBM) for x in (
            v, grid_y.T, grid_x.reshape(1, taps), test_x.reshape(1, taps), test_y.T)])
        out = jax.ShapeDtypeStruct((pairs, rows, cols), F32)
        sub, ger = pl.pallas_call(
            functools.partial(stress_kernel, margin, batch),
            out_shape=(out, out),
            in_specs=[vmem] * 6,
            out_specs=(anywhere, anywhere),
            scratch_shapes=[
                pltpu.VMEM((comps, rows_mid, wide), F32),
                pltpu.VMEM((comps, rows, cols), F32),
                pltpu.VMEM((pairs, rows, cols), F32),
                pltpu.VMEM((pairs, rows, cols), F32),
                pltpu.VMEM((slots, rows_ext + LANES, wide), BF),
                pltpu.VMEM((slots, rows_ext + LANES, wide), BF),
                pltpu.SemaphoreType.DMA((2, pairs)),
            ],
            compiler_params=pltpu.CompilerParams(vmem_limit_bytes=48 << 20),
            name="stress",
        )(ext, *weights)
        subs.append(jnp.swapaxes(sub, 1, 2))
        gers.append(jnp.swapaxes(ger, 1, 2))
    return jnp.stack(subs, axis=1), jnp.stack(gers, axis=1)


def solution(mesh):
    nx, ny = mesh.shape["gx"], mesh.shape["gy"]
    field = P(None, None, "gy", "gx")
    return jax.shard_map(
        functools.partial(local, nx, ny),
        mesh=mesh,
        in_specs=(field, P(), P("gy", None), P(), P("gy", None)),
        out_specs=(field, field),
        check_vma=False,
    )
```

```python
import functools

import jax
import jax.numpy as jnp
from jax import lax
from jax.experimental import pallas as pl
from jax.experimental.pallas import tpu as pltpu
from jax.sharding import PartitionSpec as P

MESH = pl.DeviceIdType.MESH
LANES = 128
SUB = 8
DIRECTIONS = [(1, 0), (-1, 0), (0, 1), (0, -1), (1, 1), (-1, 1), (1, -1), (-1, -1)]
BF = jnp.bfloat16
F32 = jnp.float32


def round_up(value, unit):
    return (value + unit - 1) // unit * unit


def split(value):
    high = value.astype(BF)
    return high, (value - high.astype(F32)).astype(BF)


def pair_of(p):
    first = jnp.where(p < 3, 0, jnp.where(p < 5, 1, 2))
    second = jnp.where(p < 3, p, jnp.where(p < 5, p - 2, 2))
    return first, second


def dot(a, b):
    return jnp.dot(a, b, preferred_element_type=F32)


def x_weights(w_ref, step, out):
    taps = w_ref.shape[1]
    w = jnp.concatenate([w_ref[...], jnp.zeros((1, LANES - taps), F32)], axis=1)
    w = w / jnp.sum(w)
    band = pltpu.roll(jnp.broadcast_to(w, (LANES, LANES)), 0, 1, stride=1, stride_axis=0)
    high, low = split(band[0:step])
    out[0:step, 0:LANES] = high
    out[0:step, LANES:] = high
    out[step:, 0:LANES] = low
    out[step:, LANES:] = jnp.zeros((step, LANES), BF)


def y_weights(table, taps, first_row, total, cols, main, edge=None, tiles=None):
    margin = (taps - 1) // 2
    lanes = table.shape[1]
    wide = cols + LANES
    k = lax.broadcasted_iota(jnp.int32, (LANES, lanes), 0)
    lane = lax.broadcasted_iota(jnp.int32, (LANES, lanes), 1)
    y = first_row + jnp.where(lane < cols + LANES // 2, lane, lane - wide)
    source = y + k - margin
    keep = (k < taps) & (source >= 0) & (source < total) & (y >= 0) & (y < total)
    w = jnp.where(keep, jnp.concatenate(
        [table, jnp.zeros((LANES - table.shape[0], lanes), F32)], axis=0), 0.0)
    s = jnp.sum(w, axis=0, keepdims=True)
    w = (w / jnp.where(s > 0.0, s, 1.0)).T
    zeros = jnp.zeros((LANES, cols), F32)
    for t in (range(lanes // LANES) if tiles is None else tiles):
        at = slice(t * LANES, (t + 1) * LANES)
        tile = jnp.concatenate([w[at], zeros], axis=1)
        band = pltpu.roll(tile, (t * LANES - margin) % wide, 1, stride=1, stride_axis=0)
        if t * LANES < cols:
            own, halo = band[:, 0:cols].T, band[:, cols:]
            own_high, own_low = split(own)
            main[0:cols, at] = own_high
            main[cols:2 * cols, at] = own_low
            main[2 * cols:3 * cols, at] = own_high
            high = halo.astype(BF).astype(F32)
            packed = high + pltpu.roll(high, 2 * margin, 1) + pltpu.roll(halo - high, 4 * margin, 1)
            main[3 * cols:, at] = packed.T.astype(BF)
        else:
            edge_high, edge_low = split(band.T)
            at = 0
            for lo, hi in ((0, cols), (cols, wide)):
                for part in (edge_high, edge_low, edge_high):
                    edge[at:at + hi - lo] = part[lo:hi]
                    at += hi - lo


def halo_kernel(nx, ny, width, v_hbm, t_hbm, gx_hbm, tx_hbm, ty_hbm,
                ext_ref, gxw, txw, gym, gye, tym,
                v_ref, t_ref, gx_ref, tx_ref, ty_ref, text_ref, load_sem, pack_d, pack_u, from_d, from_u, from_l, from_r, corners, t_low, t_high,
                send_sem, recv_sem):
    comps, rows, cols = v_ref.shape
    taps = t_ref.shape[0]
    margin = width // 2
    me_x, me_y = lax.axis_index("gx"), lax.axis_index("gy")

    def device(dx, dy):
        return {"gx": lax.rem(me_x + dx + nx, nx), "gy": lax.rem(me_y + dy + ny, ny)}

    barrier = pltpu.get_barrier_semaphore()
    for dx, dy in DIRECTIONS:
        pl.semaphore_signal(barrier, inc=1, device_id=device(dx, dy), device_id_type=MESH)

    loads = [pltpu.make_async_copy(src, dst, load_sem.at[i]) for i, (src, dst) in enumerate((
        (v_hbm, v_ref), (t_hbm, t_ref), (gx_hbm, gx_ref), (tx_hbm, tx_ref), (ty_hbm, ty_ref)))]
    for load in loads:
        load.start()
    per = LANES // width
    groups = rows // width
    pl.semaphore_wait(barrier, len(DIRECTIONS))
    along = [pltpu.make_async_remote_copy(
        src_ref=v_hbm.at[:, pl.ds(start, width), :], dst_ref=dst, send_sem=send_sem.at[i],
        recv_sem=recv_sem.at[i], device_id=device(dx, 0), device_id_type=MESH)
        for i, (dx, start, dst) in enumerate(((1, rows - width, from_l), (-1, 0, from_r)))]
    for copy in along:
        copy.start()
    loads[0].wait()
    for c in range(comps):
        for g in range(groups):
            for q in range(per):
                src = pl.ds(g * width + q * SUB, SUB)
                dst = pl.ds(g * SUB, SUB)
                pack_u[c, dst, q * width:(q + 1) * width] = v_ref[c, src, cols - width:cols]
                pack_d[c, dst, q * width:(q + 1) * width] = v_ref[c, src, 0:width]
    loads[1].wait()
    first, last = pl.ds(0, SUB), pl.ds((groups - 1) * SUB, SUB)
    sources = [
        pack_u, pack_d,
        pack_u.at[:, last, :], pack_u.at[:, first, :], pack_d.at[:, last, :], pack_d.at[:, first, :],
    ]
    targets = [from_d, from_u] + [corners.at[i] for i in range(4)]
    copies = [(0, copy) for copy in along]
    for i, (dx, dy) in enumerate(DIRECTIONS):
        if dy == 0:
            continue
        copies.append((dy, pltpu.make_async_remote_copy(
            src_ref=sources[i - 2], dst_ref=targets[i - 2], send_sem=send_sem.at[i],
            recv_sem=recv_sem.at[i], device_id=device(dx, dy), device_id_type=MESH)))
    for i, (dy, src, dst) in enumerate([
        (1, t_ref.at[:, pl.ds(cols - LANES, LANES)], t_low),
        (-1, t_ref.at[:, pl.ds(0, LANES)], t_high),
    ]):
        n = len(DIRECTIONS) + i
        copies.append((dy, pltpu.make_async_remote_copy(
            src_ref=src, dst_ref=dst, send_sem=send_sem.at[n],
            recv_sem=recv_sem.at[n], device_id=device(0, dy), device_id_type=MESH)))

    has_up, has_down = me_y < ny - 1, me_y > 0
    for sign, present in ((1, has_up), (-1, has_down)):
        @pl.when(present)
        def _(sign=sign):
            for dy, copy in copies:
                if dy == sign:
                    copy.start()

    rows_ext = rows + 2 * width
    ext_ref[:, :, cols:] = jnp.zeros((comps, rows_ext, LANES), F32)
    text_ref[...] = jnp.zeros_like(text_ref)
    for c in range(comps):
        ext_ref[c, pl.ds(width, rows), 0:cols] = v_ref[c]
    text_ref[0:taps, 0:cols] = t_ref[...]
    for load in loads[2:]:
        load.wait()
    first_row, total = me_y * cols, cols * ny
    x_weights(gx_ref, gxw.shape[0] // 2, gxw)
    x_weights(tx_ref, txw.shape[0] // 2, txw)
    own_tiles = range(cols // LANES)
    y_weights(t_ref[...], taps, first_row, total, cols, gym, tiles=own_tiles)
    y_weights(ty_ref[...], taps, first_row, total, cols, tym, tiles=own_tiles)

    def unpack(buf, c, row, lane, count):
        for g in range(count):
            for q in range(per):
                ext_ref[c, pl.ds(row + g * width + q * SUB, SUB), lane:lane + width] = (
                    buf[c, pl.ds(g * SUB, SUB), q * width:(q + 1) * width])

    for sign, present, lane, mid, pair, tile, at in (
        (1, has_down, cols + LANES - width, from_d, (0, 1), t_low, LANES - margin),
        (-1, has_up, cols, from_u, (2, 3), t_high, 0),
    ):
        @pl.when(present)
        def _(sign=sign, lane=lane, mid=mid, pair=pair, tile=tile, at=at):
            for dy, copy in copies:
                if dy == sign:
                    copy.wait_recv()
            for c in range(comps):
                unpack(mid, c, width, lane, groups)
                unpack(corners.at[pair[0]], c, 0, lane, 1)
                unpack(corners.at[pair[1]], c, width + rows, lane, 1)
            text_ref[0:taps, cols + at:cols + at + margin] = tile[:, at:at + margin]

    y_weights(text_ref[...], taps, first_row, total, cols, gym, gye, tiles=(cols // LANES,))
    copies[0][1].wait_recv()
    for c in range(comps):
        ext_ref[c, pl.ds(0, width), 0:cols] = from_l[c]
    copies[1][1].wait_recv()
    for c in range(comps):
        ext_ref[c, pl.ds(width + rows, width), 0:cols] = from_r[c]

    for dy, copy in copies:
        if dy == 0:
            copy.wait_send()
    for sign, present in ((1, has_up), (-1, has_down)):
        @pl.when(present)
        def _(sign=sign):
            for dy, copy in copies:
                if dy == sign:
                    copy.wait_send()


def y_filter(value, margin, cols, main, put, edge=None):
    high, low = split(value[:, 0:cols])
    halo = value[:, cols:]
    lane = lax.broadcasted_iota(jnp.int32, halo.shape, 1)
    near = jnp.where((lane < margin) | (lane >= LANES - margin), halo, 0.0)
    near_high = near.astype(BF).astype(F32)
    packed = near_high + pltpu.roll(near - near_high, 2 * margin, 1) + pltpu.roll(near_high, 4 * margin, 1)
    put(dot(jnp.concatenate([high, high, low, packed.astype(BF)], axis=1), main[...]), slice(0, cols))
    if edge is not None:
        hh, hl = split(halo)
        put(dot(jnp.concatenate([high, high, low, hh, hh, hl], axis=1), edge[...]),
            slice(cols, cols + LANES))


def x_filter(zh, zl, start, count, lanes, weights, put):
    step = weights.shape[0] // 2
    for s in range(0, count, step):
        size = min(step, count - s)
        at = slice(start + s, start + s + LANES)
        data = jnp.concatenate([zh[at, lanes], zl[at, lanes]], axis=0)
        if size == step:
            r = dot(weights[...], data)
        else:
            r = dot(jnp.concatenate([weights[0:size], weights[step:step + size]], axis=0), data)
        put(s, size, r[0:size] + r[size:])


def stress_kernel(margin, batch, ext_ref, gxw, txw, gym, gye, tym, sub_ref, ger_ref,
                  coarse, tested, sub, ger, zh, zl, sems):
    comps, rows_ext, wide = ext_ref.shape
    pairs, rows, cols = sub_ref.shape
    rows_mid = rows + 2 * margin
    own = slice(0, cols)
    everything = slice(0, wide)
    for slot in range(zh.shape[0]):
        zh[slot, pl.ds(rows_ext, LANES), :] = jnp.zeros((LANES, wide), BF)
        zl[slot, pl.ds(rows_ext, LANES), :] = jnp.zeros((LANES, wide), BF)

    def store(slot, n, count):
        def put(z, lanes):
            high, low = split(z)
            for b in range(n):
                at = slice(b * count, (b + 1) * count)
                zh[slot + b, 0:count, lanes], zl[slot + b, 0:count, lanes] = high[at], low[at]
        return put

    def stacked(values):
        return jnp.concatenate(values, axis=0)

    y_filter(stacked([ext_ref[c] for c in range(comps)]), margin, cols, gym,
             store(0, comps, rows_ext), gye)
    for c in range(comps):
        def put(start, size, value, c=c):
            coarse[c, pl.ds(start, size), :] = value

        x_filter(zh.at[c], zl.at[c], 0, rows_mid, everything, gxw, put)
    y_filter(stacked([coarse[c] for c in range(comps)]), margin, cols, tym,
             store(0, comps, rows_mid))
    for c in range(comps):
        def put_tested(start, size, value, c=c):
            tested[c, pl.ds(start, size), :] = value

        x_filter(zh.at[c], zl.at[c], 0, rows, own, txw, put_tested)

    def leave(which, source, target, p):
        return pltpu.make_async_copy(source.at[p], target.at[p], sems.at[which, p])

    mid = pl.ds(margin, rows_mid)

    @pl.loop(0, pairs // batch)
    def _(step):
        indices = [(step * batch + b,) + pair_of(step * batch + b) for b in range(batch)]
        y_filter(stacked([ext_ref[i, mid, :] * ext_ref[j, mid, :] for _, i, j in indices]),
                 margin, cols, gym, store(0, batch, rows_mid))
        y_filter(stacked([coarse[i] * coarse[j] for _, i, j in indices]),
                 margin, cols, tym, store(batch, batch, rows_mid))
        for b, (p, i, j) in enumerate(indices):
            def put_sub(start, size, value, p=p, i=i, j=j):
                at = pl.ds(margin + start, size)
                sub[p, pl.ds(start, size), :] = value - coarse[i, at, own] * coarse[j, at, own]

            x_filter(zh.at[b], zl.at[b], 0, rows, own, gxw, put_sub)
        for b, (p, i, j) in enumerate(indices):
            def put_ger(start, size, value, p=p, i=i, j=j):
                at = pl.ds(start, size)
                ger[p, at, :] = value - tested[i, at, :] * tested[j, at, :]

            x_filter(zh.at[batch + b], zl.at[batch + b], 0, rows, own, txw, put_ger)
        for p, _, _ in indices:
            leave(0, sub, sub_ref, p).start()
            leave(1, ger, ger_ref, p).start()

    @pl.loop(0, pairs)
    def _(p):
        leave(0, sub, sub_ref, p).wait()
        leave(1, ger, ger_ref, p).wait()


def local(nx, ny, velocity, grid_x, grid_y, test_x, test_y):
    comps, planes, cols, rows = velocity.shape
    taps = grid_x.shape[0]
    margin = (taps - 1) // 2
    width = 2 * margin
    wide = cols + LANES
    step = LANES - width
    pairs = comps * (comps + 1) // 2
    batch = 2
    slots = max(comps, 2 * batch)
    vmem = pl.BlockSpec(memory_space=pltpu.VMEM)
    anywhere = pl.BlockSpec(memory_space=pl.ANY)
    packed = rows // width * SUB
    subs, gers = [], []
    rows_mid, rows_ext = rows + width, rows + 2 * width
    for plane in range(planes):
        v = jnp.swapaxes(velocity[:, plane], 1, 2)
        ext, *weights = pl.pallas_call(
            functools.partial(halo_kernel, nx, ny, width),
            out_shape=(
                jax.ShapeDtypeStruct((comps, rows_ext, wide), F32),
                jax.ShapeDtypeStruct((2 * step, 2 * LANES), BF),
                jax.ShapeDtypeStruct((2 * step, 2 * LANES), BF),
                jax.ShapeDtypeStruct((3 * cols + LANES, cols), BF),
                jax.ShapeDtypeStruct((3 * wide, LANES), BF),
                jax.ShapeDtypeStruct((3 * cols + LANES, cols), BF),
            ),
            in_specs=[pl.BlockSpec(memory_space=pltpu.HBM)] * 5,
            out_specs=(vmem,) * 6,
            scratch_shapes=[
                pltpu.VMEM((comps, rows, cols), F32),
                pltpu.VMEM((taps, cols), F32),
                pltpu.VMEM((1, taps), F32),
                pltpu.VMEM((1, taps), F32),
                pltpu.VMEM((taps, cols), F32),
                pltpu.VMEM((round_up(taps, SUB), wide), F32),
                pltpu.SemaphoreType.DMA((5,)),
                pltpu.VMEM((comps, packed, LANES), F32),
                pltpu.VMEM((comps, packed, LANES), F32),
                pltpu.VMEM((comps, packed, LANES), F32),
                pltpu.VMEM((comps, packed, LANES), F32),
                pltpu.VMEM((comps, width, cols), F32),
                pltpu.VMEM((comps, width, cols), F32),
                pltpu.VMEM((4, comps, SUB, LANES), F32),
                pltpu.VMEM((taps, LANES), F32),
                pltpu.VMEM((taps, LANES), F32),
                pltpu.SemaphoreType.DMA((len(DIRECTIONS) + 2,)),
                pltpu.SemaphoreType.DMA((len(DIRECTIONS) + 2,)),
            ],
            compiler_params=pltpu.CompilerParams(
                collective_id=plane, has_side_effects=True, vmem_limit_bytes=48 << 20),
            name="halo",
        )(*[pltpu.with_memory_space_constraint(x, pltpu.HBM) for x in (
            v, grid_y.T, grid_x.reshape(1, taps), test_x.reshape(1, taps), test_y.T)])
        out = jax.ShapeDtypeStruct((pairs, rows, cols), F32)
        sub, ger = pl.pallas_call(
            functools.partial(stress_kernel, margin, batch),
            out_shape=(out, out),
            in_specs=[vmem] * 6,
            out_specs=(anywhere, anywhere),
            scratch_shapes=[
                pltpu.VMEM((comps, rows_mid, wide), F32),
                pltpu.VMEM((comps, rows, cols), F32),
                pltpu.VMEM((pairs, rows, cols), F32),
                pltpu.VMEM((pairs, rows, cols), F32),
                pltpu.VMEM((slots, rows_ext + LANES, wide), BF),
                pltpu.VMEM((slots, rows_ext + LANES, wide), BF),
                pltpu.SemaphoreType.DMA((2, pairs)),
            ],
            compiler_params=pltpu.CompilerParams(vmem_limit_bytes=48 << 20),
            name="stress",
        )(ext, *weights)
        subs.append(jnp.swapaxes(sub, 1, 2))
        gers.append(jnp.swapaxes(ger, 1, 2))
    return jnp.stack(subs, axis=1), jnp.stack(gers, axis=1)


def solution(mesh):
    nx, ny = mesh.shape["gx"], mesh.shape["gy"]
    field = P(None, None, "gy", "gx")
    return jax.shard_map(
        functools.partial(local, nx, ny),
        mesh=mesh,
        in_specs=(field, P(), P("gy", None), P(), P("gy", None)),
        out_specs=(field, field),
        check_vma=False,
    )
```

```python
import functools

import jax
import jax.numpy as jnp
from jax import lax
from jax.experimental import pallas as pl
from jax.experimental.pallas import tpu as pltpu
from jax.sharding import PartitionSpec as P

MESH = pl.DeviceIdType.MESH
LANES = 128
SUB = 8
DIRECTIONS = [(1, 0), (-1, 0), (0, 1), (0, -1), (1, 1), (-1, 1), (1, -1), (-1, -1)]
BF = jnp.bfloat16
F32 = jnp.float32


def round_up(value, unit):
    return (value + unit - 1) // unit * unit


def split(value):
    high = value.astype(BF)
    return high, (value - high.astype(F32)).astype(BF)


def pair_of(p):
    first = jnp.where(p < 3, 0, jnp.where(p < 5, 1, 2))
    second = jnp.where(p < 3, p, jnp.where(p < 5, p - 2, 2))
    return first, second


def dot(a, b):
    return jnp.dot(a, b, preferred_element_type=F32)


def x_weights(w_ref, step, out):
    taps = w_ref.shape[1]
    w = jnp.concatenate([w_ref[...], jnp.zeros((1, LANES - taps), F32)], axis=1)
    w = w / jnp.sum(w)
    band = pltpu.roll(jnp.broadcast_to(w, (LANES, LANES)), 0, 1, stride=1, stride_axis=0)
    high, low = split(band[0:step])
    out[0:step, 0:LANES] = high
    out[0:step, LANES:] = high
    out[step:, 0:LANES] = low
    out[step:, LANES:] = jnp.zeros((step, LANES), BF)


def y_weights(table, taps, first_row, total, cols, main, edge=None, tiles=None):
    margin = (taps - 1) // 2
    lanes = table.shape[1]
    wide = cols + LANES
    k = lax.broadcasted_iota(jnp.int32, (LANES, lanes), 0)
    lane = lax.broadcasted_iota(jnp.int32, (LANES, lanes), 1)
    y = first_row + jnp.where(lane < cols + LANES // 2, lane, lane - wide)
    source = y + k - margin
    keep = (k < taps) & (source >= 0) & (source < total) & (y >= 0) & (y < total)
    w = jnp.where(keep, jnp.concatenate(
        [table, jnp.zeros((LANES - table.shape[0], lanes), F32)], axis=0), 0.0)
    s = jnp.sum(w, axis=0, keepdims=True)
    w = (w / jnp.where(s > 0.0, s, 1.0)).T
    zeros = jnp.zeros((LANES, cols), F32)
    for t in (range(lanes // LANES) if tiles is None else tiles):
        at = slice(t * LANES, (t + 1) * LANES)
        tile = jnp.concatenate([w[at], zeros], axis=1)
        band = pltpu.roll(tile, (t * LANES - margin) % wide, 1, stride=1, stride_axis=0)
        if t * LANES < cols:
            own, halo = band[:, 0:cols].T, band[:, cols:]
            own_high, own_low = split(own)
            main[0:cols, at] = own_high
            main[cols:2 * cols, at] = own_low
            main[2 * cols:3 * cols, at] = own_high
            high = halo.astype(BF).astype(F32)
            packed = high + pltpu.roll(high, 2 * margin, 1) + pltpu.roll(halo - high, 4 * margin, 1)
            main[3 * cols:, at] = packed.T.astype(BF)
        else:
            edge_high, edge_low = split(band.T)
            at = 0
            for lo, hi in ((0, cols), (cols, wide)):
                for part in (edge_high, edge_low, edge_high):
                    edge[at:at + hi - lo] = part[lo:hi]
                    at += hi - lo


def y_filter(value, margin, cols, main, put, edge=None):
    high, low = split(value[:, 0:cols])
    halo = value[:, cols:]
    lane = lax.broadcasted_iota(jnp.int32, halo.shape, 1)
    near = jnp.where((lane < margin) | (lane >= LANES - margin), halo, 0.0)
    near_high = near.astype(BF).astype(F32)
    packed = near_high + pltpu.roll(near - near_high, 2 * margin, 1) + pltpu.roll(near_high, 4 * margin, 1)
    put(dot(jnp.concatenate([high, high, low, packed.astype(BF)], axis=1), main[...]), slice(0, cols))
    if edge is not None:
        hh, hl = split(halo)
        put(dot(jnp.concatenate([high, high, low, hh, hh, hl], axis=1), edge[...]),
            slice(cols, cols + LANES))


def halo_kernel(nx, ny, width, v_hbm, t_hbm, gx_hbm, tx_hbm, ty_hbm,
                zch, zcl, zph, zpl, gxw, txw, tym,
                ext_ref, gym, gye, v_ref, t_ref, gx_ref, tx_ref, ty_ref, text_ref, load_sem, pack_d, pack_u, from_d, from_u, from_l, from_r, corners, t_low, t_high,
                send_sem, recv_sem):
    comps, rows, cols = v_ref.shape
    taps = t_ref.shape[0]
    margin = width // 2
    me_x, me_y = lax.axis_index("gx"), lax.axis_index("gy")

    def device(dx, dy):
        return {"gx": lax.rem(me_x + dx + nx, nx), "gy": lax.rem(me_y + dy + ny, ny)}

    barrier = pltpu.get_barrier_semaphore()
    for dx, dy in DIRECTIONS:
        pl.semaphore_signal(barrier, inc=1, device_id=device(dx, dy), device_id_type=MESH)

    loads = [pltpu.make_async_copy(src, dst, load_sem.at[i]) for i, (src, dst) in enumerate((
        (v_hbm, v_ref), (t_hbm, t_ref), (gx_hbm, gx_ref), (tx_hbm, tx_ref), (ty_hbm, ty_ref)))]
    for load in loads:
        load.start()
    per = LANES // width
    groups = rows // width
    pl.semaphore_wait(barrier, len(DIRECTIONS))
    along = [pltpu.make_async_remote_copy(
        src_ref=v_hbm.at[:, pl.ds(start, width), :], dst_ref=dst, send_sem=send_sem.at[i],
        recv_sem=recv_sem.at[i], device_id=device(dx, 0), device_id_type=MESH)
        for i, (dx, start, dst) in enumerate(((1, rows - width, from_l), (-1, 0, from_r)))]
    for copy in along:
        copy.start()
    loads[0].wait()
    for c in range(comps):
        for g in range(groups):
            for q in range(per):
                src = pl.ds(g * width + q * SUB, SUB)
                dst = pl.ds(g * SUB, SUB)
                pack_u[c, dst, q * width:(q + 1) * width] = v_ref[c, src, cols - width:cols]
                pack_d[c, dst, q * width:(q + 1) * width] = v_ref[c, src, 0:width]
    loads[1].wait()
    first, last = pl.ds(0, SUB), pl.ds((groups - 1) * SUB, SUB)
    sources = [
        pack_u, pack_d,
        pack_u.at[:, last, :], pack_u.at[:, first, :], pack_d.at[:, last, :], pack_d.at[:, first, :],
    ]
    targets = [from_d, from_u] + [corners.at[i] for i in range(4)]
    copies = [(0, copy) for copy in along]
    for i, (dx, dy) in enumerate(DIRECTIONS):
        if dy == 0:
            continue
        copies.append((dy, pltpu.make_async_remote_copy(
            src_ref=sources[i - 2], dst_ref=targets[i - 2], send_sem=send_sem.at[i],
            recv_sem=recv_sem.at[i], device_id=device(dx, dy), device_id_type=MESH)))
    for i, (dy, src, dst) in enumerate([
        (1, t_ref.at[:, pl.ds(cols - LANES, LANES)], t_low),
        (-1, t_ref.at[:, pl.ds(0, LANES)], t_high),
    ]):
        n = len(DIRECTIONS) + i
        copies.append((dy, pltpu.make_async_remote_copy(
            src_ref=src, dst_ref=dst, send_sem=send_sem.at[n],
            recv_sem=recv_sem.at[n], device_id=device(0, dy), device_id_type=MESH)))

    has_up, has_down = me_y < ny - 1, me_y > 0
    for sign, present in ((1, has_up), (-1, has_down)):
        @pl.when(present)
        def _(sign=sign):
            for dy, copy in copies:
                if dy == sign:
                    copy.start()

    rows_ext = rows + 2 * width
    ext_ref[:, :, cols:] = jnp.zeros((comps, rows_ext, LANES), F32)
    text_ref[...] = jnp.zeros_like(text_ref)
    for c in range(comps):
        ext_ref[c, pl.ds(width, rows), 0:cols] = v_ref[c]
    text_ref[0:taps, 0:cols] = t_ref[...]
    for load in loads[2:]:
        load.wait()
    first_row, total = me_y * cols, cols * ny
    x_weights(gx_ref, gxw.shape[0] // 2, gxw)
    x_weights(tx_ref, txw.shape[0] // 2, txw)
    own_tiles = range(cols // LANES)
    y_weights(t_ref[...], taps, first_row, total, cols, gym, tiles=own_tiles)
    y_weights(ty_ref[...], taps, first_row, total, cols, tym, tiles=own_tiles)

    def unpack(buf, c, row, lane, count):
        for g in range(count):
            for q in range(per):
                ext_ref[c, pl.ds(row + g * width + q * SUB, SUB), lane:lane + width] = (
                    buf[c, pl.ds(g * SUB, SUB), q * width:(q + 1) * width])

    for sign, present, lane, mid, pair, tile, at in (
        (1, has_down, cols + LANES - width, from_d, (0, 1), t_low, LANES - margin),
        (-1, has_up, cols, from_u, (2, 3), t_high, 0),
    ):
        @pl.when(present)
        def _(sign=sign, lane=lane, mid=mid, pair=pair, tile=tile, at=at):
            for dy, copy in copies:
                if dy == sign:
                    copy.wait_recv()
            for c in range(comps):
                unpack(mid, c, width, lane, groups)
                unpack(corners.at[pair[0]], c, 0, lane, 1)
                unpack(corners.at[pair[1]], c, width + rows, lane, 1)
            text_ref[0:taps, cols + at:cols + at + margin] = tile[:, at:at + margin]

    y_weights(text_ref[...], taps, first_row, total, cols, gym, gye, tiles=(cols // LANES,))

    def store(high_ref, low_ref, places, count):
        def put(z, lanes):
            high, low = split(z)
            for n, (slot, row) in enumerate(places):
                at = slice(n * count, (n + 1) * count)
                high_ref[slot, pl.ds(row, count), lanes] = high[at]
                low_ref[slot, pl.ds(row, count), lanes] = low[at]
        return put

    def stacked(values):
        return jnp.concatenate(values, axis=0)

    combos = [(i, j) for i in range(comps) for j in range(i, comps)]
    for ref, tail in ((zch, rows_ext), (zcl, rows_ext), (zph, rows_ext - width), (zpl, rows_ext - width)):
        ref[:, pl.ds(tail, LANES), :] = jnp.zeros((ref.shape[0], LANES, ref.shape[2]), BF)
    body = pl.ds(width, rows)
    y_filter(stacked([ext_ref[c, body, :] for c in range(comps)]), margin, cols, gym,
             store(zch, zcl, [(c, width) for c in range(comps)], rows), gye)
    for start in range(0, len(combos), 2):
        some = list(enumerate(combos))[start:start + 2]
        y_filter(stacked([ext_ref[i, body, :] * ext_ref[j, body, :] for _, (i, j) in some]), margin,
                 cols, gym, store(zph, zpl, [(p, margin) for p, _ in some], rows))

    copies[0][1].wait_recv()
    for c in range(comps):
        ext_ref[c, pl.ds(0, width), 0:cols] = from_l[c]
    copies[1][1].wait_recv()
    for c in range(comps):
        ext_ref[c, pl.ds(width + rows, width), 0:cols] = from_r[c]
    ends = [(0, 0), (width + rows, width + rows)]
    y_filter(stacked([ext_ref[c, pl.ds(at, width), :] for c in range(comps) for at, _ in ends]),
             margin, cols, gym,
             store(zch, zcl, [(c, to) for c in range(comps) for _, to in ends], width), gye)
    ends = [(margin, 0), (width + rows, margin + rows)]
    y_filter(stacked([ext_ref[i, pl.ds(at, margin), :] * ext_ref[j, pl.ds(at, margin), :]
                      for i, j in combos for at, _ in ends]), margin, cols, gym,
             store(zph, zpl, [(p, to) for p in range(len(combos)) for _, to in ends], margin))

    for dy, copy in copies:
        if dy == 0:
            copy.wait_send()
    for sign, present in ((1, has_up), (-1, has_down)):
        @pl.when(present)
        def _(sign=sign):
            for dy, copy in copies:
                if dy == sign:
                    copy.wait_send()


def x_filter(zh, zl, start, count, lanes, weights, put):
    step = weights.shape[0] // 2
    for s in range(0, count, step):
        size = min(step, count - s)
        at = slice(start + s, start + s + LANES)
        data = jnp.concatenate([zh[at, lanes], zl[at, lanes]], axis=0)
        if size == step:
            r = dot(weights[...], data)
        else:
            r = dot(jnp.concatenate([weights[0:size], weights[step:step + size]], axis=0), data)
        put(s, size, r[0:size] + r[size:])


def stress_kernel(margin, batch, zch, zcl, zph, zpl, gxw, txw, tym, sub_ref, ger_ref,
                  coarse, tested, sub, ger, zh, zl, sems):
    comps, wide = zch.shape[0], zch.shape[2]
    pairs, rows, cols = sub_ref.shape
    rows_mid = rows + 2 * margin
    own = slice(0, cols)
    everything = slice(0, wide)
    for slot in range(zh.shape[0]):
        zh[slot, pl.ds(rows_mid, LANES), :] = jnp.zeros((LANES, cols), BF)
        zl[slot, pl.ds(rows_mid, LANES), :] = jnp.zeros((LANES, cols), BF)

    def store(slot, n, count):
        def put(z, lanes):
            high, low = split(z)
            for b in range(n):
                at = slice(b * count, (b + 1) * count)
                zh[slot + b, 0:count, lanes], zl[slot + b, 0:count, lanes] = high[at], low[at]
        return put

    def stacked(values):
        return jnp.concatenate(values, axis=0)

    for c in range(comps):
        def put(start, size, value, c=c):
            coarse[c, pl.ds(start, size), :] = value

        x_filter(zch.at[c], zcl.at[c], 0, rows_mid, everything, gxw, put)
    y_filter(stacked([coarse[c] for c in range(comps)]), margin, cols, tym,
             store(0, comps, rows_mid))
    for c in range(comps):
        def put_tested(start, size, value, c=c):
            tested[c, pl.ds(start, size), :] = value

        x_filter(zh.at[c], zl.at[c], 0, rows, own, txw, put_tested)

    def leave(which, source, target, p):
        return pltpu.make_async_copy(source.at[p], target.at[p], sems.at[which, p])

    @pl.loop(0, pairs // batch)
    def _(step):
        indices = [(step * batch + b,) + pair_of(step * batch + b) for b in range(batch)]
        y_filter(stacked([coarse[i] * coarse[j] for _, i, j in indices]),
                 margin, cols, tym, store(0, batch, rows_mid))
        for b, (p, i, j) in enumerate(indices):
            def put_sub(start, size, value, p=p, i=i, j=j):
                at = pl.ds(margin + start, size)
                sub[p, pl.ds(start, size), :] = value - coarse[i, at, own] * coarse[j, at, own]

            x_filter(zph.at[p], zpl.at[p], 0, rows, own, gxw, put_sub)
        for b, (p, i, j) in enumerate(indices):
            def put_ger(start, size, value, p=p, i=i, j=j):
                at = pl.ds(start, size)
                ger[p, at, :] = value - tested[i, at, :] * tested[j, at, :]

            x_filter(zh.at[b], zl.at[b], 0, rows, own, txw, put_ger)
        for p, _, _ in indices:
            leave(0, sub, sub_ref, p).start()
            leave(1, ger, ger_ref, p).start()

    @pl.loop(0, pairs)
    def _(p):
        leave(0, sub, sub_ref, p).wait()
        leave(1, ger, ger_ref, p).wait()


def local(nx, ny, velocity, grid_x, grid_y, test_x, test_y):
    comps, planes, cols, rows = velocity.shape
    taps = grid_x.shape[0]
    margin = (taps - 1) // 2
    width = 2 * margin
    wide = cols + LANES
    step = LANES - width
    pairs = comps * (comps + 1) // 2
    batch = 2
    slots = max(comps, batch)
    vmem = pl.BlockSpec(memory_space=pltpu.VMEM)
    anywhere = pl.BlockSpec(memory_space=pl.ANY)
    packed = rows // width * SUB
    subs, gers = [], []
    rows_mid, rows_ext = rows + width, rows + 2 * width
    for plane in range(planes):
        v = jnp.swapaxes(velocity[:, plane], 1, 2)
        middle = pl.pallas_call(
            functools.partial(halo_kernel, nx, ny, width),
            out_shape=(
                jax.ShapeDtypeStruct((comps, rows_ext + LANES, wide), BF),
                jax.ShapeDtypeStruct((comps, rows_ext + LANES, wide), BF),
                jax.ShapeDtypeStruct((pairs, rows_mid + LANES, cols), BF),
                jax.ShapeDtypeStruct((pairs, rows_mid + LANES, cols), BF),
                jax.ShapeDtypeStruct((2 * step, 2 * LANES), BF),
                jax.ShapeDtypeStruct((2 * step, 2 * LANES), BF),
                jax.ShapeDtypeStruct((3 * cols + LANES, cols), BF),
            ),
            in_specs=[pl.BlockSpec(memory_space=pltpu.HBM)] * 5,
            out_specs=(vmem,) * 7,
            scratch_shapes=[
                pltpu.VMEM((comps, rows_ext, wide), F32),
                pltpu.VMEM((3 * cols + LANES, cols), BF),
                pltpu.VMEM((3 * wide, LANES), BF),
                pltpu.VMEM((comps, rows, cols), F32),
                pltpu.VMEM((taps, cols), F32),
                pltpu.VMEM((1, taps), F32),
                pltpu.VMEM((1, taps), F32),
                pltpu.VMEM((taps, cols), F32),
                pltpu.VMEM((round_up(taps, SUB), wide), F32),
                pltpu.SemaphoreType.DMA((5,)),
                pltpu.VMEM((comps, packed, LANES), F32),
                pltpu.VMEM((comps, packed, LANES), F32),
                pltpu.VMEM((comps, packed, LANES), F32),
                pltpu.VMEM((comps, packed, LANES), F32),
                pltpu.VMEM((comps, width, cols), F32),
                pltpu.VMEM((comps, width, cols), F32),
                pltpu.VMEM((4, comps, SUB, LANES), F32),
                pltpu.VMEM((taps, LANES), F32),
                pltpu.VMEM((taps, LANES), F32),
                pltpu.SemaphoreType.DMA((len(DIRECTIONS) + 2,)),
                pltpu.SemaphoreType.DMA((len(DIRECTIONS) + 2,)),
            ],
            compiler_params=pltpu.CompilerParams(
                collective_id=plane, has_side_effects=True, vmem_limit_bytes=40 << 20),
            name="halo",
        )(*[pltpu.with_memory_space_constraint(x, pltpu.HBM) for x in (
            v, grid_y.T, grid_x.reshape(1, taps), test_x.reshape(1, taps), test_y.T)])
        out = jax.ShapeDtypeStruct((pairs, rows, cols), F32)
        sub, ger = pl.pallas_call(
            functools.partial(stress_kernel, margin, batch),
            out_shape=(out, out),
            in_specs=[vmem] * 7,
            out_specs=(anywhere, anywhere),
            scratch_shapes=[
                pltpu.VMEM((comps, rows_mid, wide), F32),
                pltpu.VMEM((comps, rows, cols), F32),
                pltpu.VMEM((pairs, rows, cols), F32),
                pltpu.VMEM((pairs, rows, cols), F32),
                pltpu.VMEM((slots, rows_mid + LANES, cols), BF),
                pltpu.VMEM((slots, rows_mid + LANES, cols), BF),
                pltpu.SemaphoreType.DMA((2, pairs)),
            ],
            compiler_params=pltpu.CompilerParams(vmem_limit_bytes=44 << 20),
            name="stress",
        )(*middle)
        subs.append(jnp.swapaxes(sub, 1, 2))
        gers.append(jnp.swapaxes(ger, 1, 2))
    return jnp.stack(subs, axis=1), jnp.stack(gers, axis=1)


def solution(mesh):
    nx, ny = mesh.shape["gx"], mesh.shape["gy"]
    field = P(None, None, "gy", "gx")
    return jax.shard_map(
        functools.partial(local, nx, ny),
        mesh=mesh,
        in_specs=(field, P(), P("gy", None), P(), P("gy", None)),
        out_specs=(field, field),
        check_vma=False,
    )
```
